1024 devices in a mesh: ctx: 16 (over y, x), pipe: 64 (over z, core).
Axes of the slice: x: 4, y: 4, z: 32, core: 2. Of those that a mesh axis runs over, the one named last changes fastest.
Arguments:
- q_in: bfloat16 [64, 4096, 128], P('pipe', 'ctx'), may hold values from -6 to 6
- k_in: bfloat16 [64, 4096, 128], P('pipe', 'ctx'), may hold values from -6 to 6
- v_in: bfloat16 [64, 4096, 1024], P('pipe', 'ctx'), may hold values from -6 to 6
- gate_in: bfloat16 [64, 4096, 1024], P('pipe', 'ctx'), may hold values from -6 to 6
- out_grad: bfloat16 [64, 4096, 1024], P('pipe', 'ctx'), may hold values from -6 to 6
- conv_weight: bfloat16 [64, 3, 1024], P('pipe'), may hold values from -3.5 to 3.5
- bounds: int32 [64, 16], P('pipe'), may hold values from 0 to 256, as said below
Outputs:
- q_grad: bfloat16 [64, 4096, 128], P('pipe', 'ctx')
- k_grad: bfloat16 [64, 4096, 128], P('pipe', 'ctx')
- v_grad: bfloat16 [64, 4096, 1024], P('pipe', 'ctx')
- gate_grad: bfloat16 [64, 4096, 1024], P('pipe', 'ctx')
The draws below stay inside these ranges and needn't reach their ends.
Inputs may be any that keep to these rules, and one draw needn't show every extreme that they name: bounds[s, c] is the offset within slice c of section s's sequence (of 256 tokens) at which a new document begins, or 256 where none begins at an offset of that slice; in slice 0 a document begins at offset 0 whatever bounds[s, 0] holds.
All inputs are finite; a program needn't handle non-finite values.
Results may differ from the reference program's by a relative error of at most 0.0015.
Values may be sent and summed in bfloat16 or wider, within the bound.
A program may use at most 128 MiB of HBM per device.

```python
import jax
import jax.numpy as jnp
from jax import lax

HEADS = 8
F = 16
DV = 128
CONV = 3
TOK_DEV = 256
E = 273
SECTIONS = 64
SLICES = 16
TOKENS = 4096


def draw_bounds(key, part):
    first_key, second_key, third_key = jax.random.split(jax.random.fold_in(key, 17), 3)
    picks = jax.random.randint(first_key, (SECTIONS, SLICES), 0, 3 * TOK_DEV)
    offsets = jnp.minimum(picks, TOK_DEV)
    row_pick = jax.random.randint(second_key, (), 0, SECTIONS)
    col_pick = jax.random.randint(third_key, (), 0, SLICES)
    marked = (jnp.arange(SECTIONS)[:, None] == row_pick) & (jnp.arange(SLICES)[None, :] == col_pick)
    return jnp.where(marked, 0, offsets).astype(jnp.int32)


def steps_of(rng, extent, pieces, least, largest):
    level = 1.0
    for dim, shards_of in pieces:
        steps = jax.random.uniform(jax.random.fold_in(jax.random.fold_in(rng, 6), dim), (shards_of,), jnp.float32, least / len(pieces), largest / len(pieces))
        level = level * jnp.repeat(jnp.exp(steps), extent[dim] // shards_of).reshape((-1,) + (1,) * (len(extent) - 1 - dim))
    return level


def scatter_about(own_key, dims, deviation, most, shards=(), dtype=jnp.bfloat16):
    gain = steps_of(own_key, dims, shards, -0.22, 0.18) if shards else 1.0
    result = jax.random.normal(own_key, dims, jnp.float32) * deviation * gain
    return jnp.minimum(jnp.maximum(result, -most), most).astype(dtype)


def setup_inputs(seed: int = 0) -> dict:
    seeds = jax.random.split(jax.random.key(seed), 8)
    return {
        "q_in": scatter_about(seeds[0], (SECTIONS, TOKENS, HEADS * F), 1.0, 6.0, ((0, 64), (1, 16))),
        "k_in": scatter_about(seeds[1], (SECTIONS, TOKENS, HEADS * F), 1.0, 6.0, ((0, 64), (1, 16))),
        "v_in": scatter_about(seeds[2], (SECTIONS, TOKENS, HEADS * DV), 1.0, 6.0, ((0, 64), (1, 16))),
        "gate_in": scatter_about(seeds[3], (SECTIONS, TOKENS, HEADS * DV), 1.0, 6.0, ((0, 64), (1, 16))),
        "out_grad": scatter_about(seeds[4], (SECTIONS, TOKENS, HEADS * DV), 1.0, 6.0, ((0, 64), (1, 16))),
        "conv_weight": scatter_about(seeds[5], (SECTIONS, CONV, HEADS * DV), CONV ** -0.5, 3.5, ((0, 64),)),
        "bounds": draw_bounds(jax.random.fold_in(seeds[7], 71), 0),
    }


half_root = 0.7071067811865476
highest = lax.Precision.HIGHEST

def expand_features(inputs):
    width = inputs.shape[-1]
    outer = (inputs[..., :, None] * inputs[..., None, :]).reshape(inputs.shape[:-1] + (width * width,))
    ones_col = jnp.ones(inputs.shape[:-1] + (1,), jnp.float32)
    return jnp.concatenate([ones_col, inputs, outer * half_root], axis=-1)

def section_forward(q_in, k_in, v_in, gate_in, conv_weight, bounds):
    qk_scale = F ** (-0.25)
    queries = q_in.astype(jnp.float32).reshape(SLICES, TOK_DEV, HEADS, F) * qk_scale
    keys_scaled = k_in.astype(jnp.float32).reshape(SLICES, TOK_DEV, HEADS, F) * qk_scale
    values = v_in.astype(jnp.float32).reshape(SLICES, TOK_DEV, HEADS, DV)
    position = jnp.arange(TOK_DEV).astype(jnp.int32)

    def slice_step(carry, item):
        state, norm = carry
        query_block, key_block, value_block, boundary = item
        opening = boundary % TOK_DEV
        before_doc = (position < boundary).astype(jnp.float32)
        after_doc = (position >= opening).astype(jnp.float32)
        in_newdoc = position >= boundary
        causal_mask = (position[:, None] >= position[None, :]) & (in_newdoc[:, None] == in_newdoc[None, :])
        carried = (boundary == TOK_DEV).astype(jnp.float32)
        query_phi = expand_features(query_block)
        key_phi = expand_features(key_block)
        affine = jnp.einsum('thf,shf->hts', query_block, key_block, precision=highest)
        kernel = jnp.where(causal_mask[None], 1.0 + affine + 0.5 * affine * affine, 0.0)
        numerator = jnp.einsum('hts,shd->thd', kernel, value_block, precision=highest) + before_doc[:, None, None] * jnp.einsum('the,hed->thd', query_phi, state, precision=highest)
        denominator = lax.optimization_barrier(jnp.sum(kernel, axis=2)).T + before_doc[:, None] * jnp.einsum('the,he->th', query_phi, norm, precision=highest)
        attended = numerator / denominator[:, :, None]
        key_used = key_phi * after_doc[:, None, None]
        new_state = carried * state + jnp.einsum('the,thd->hed', key_used, value_block, precision=highest)
        new_norm = carried * norm + lax.optimization_barrier(jnp.sum(key_used, axis=0))
        return ((new_state, new_norm), attended)
    start_carry = (jnp.zeros((HEADS, E, DV), jnp.float32), jnp.zeros((HEADS, E), jnp.float32))
    final_carry, attended = lax.scan(slice_step, start_carry, (queries, keys_scaled, values, bounds))
    attended = attended.reshape(SLICES * TOK_DEV, HEADS * DV)
    flags = (bounds < TOK_DEV).astype(jnp.int32)
    running = jnp.cumsum(flags)
    doc_ids = (running[:, None] - flags[:, None] * (position[None, :] < bounds[:, None]).astype(jnp.int32)).reshape(SLICES * TOK_DEV)
    gate_rows = gate_in.astype(jnp.float32)
    taps = conv_weight.astype(jnp.float32)
    mixed = taps[0] * gate_rows
    for shift_by in range(1, CONV):
        moved = jnp.concatenate([jnp.zeros((shift_by, HEADS * DV), jnp.float32), gate_rows[:-shift_by]], axis=0)
        earlier_ids = jnp.concatenate([jnp.full((shift_by,), -1, jnp.int32), doc_ids[:-shift_by]], axis=0)
        same_doc = (earlier_ids == doc_ids).astype(jnp.float32)
        mixed = mixed + taps[shift_by] * moved * same_doc[:, None]
    return attended * jax.nn.silu(mixed)

def reference(q_in, k_in, v_in, gate_in, out_grad, conv_weight, bounds):
    incoming = jnp.roll(out_grad, -1, axis=0).astype(jnp.float32)

    def one_section(item):
        query_arg, key_arg, value_arg, gate_arg, cotangent, taps, section_bounds = item

        def forward(query_in, key_in, value_in, gate_value):
            return section_forward(query_in, key_in, value_in, gate_value, taps, section_bounds)
        primal, pullback = jax.vjp(forward, query_arg, key_arg, value_arg, gate_arg)
        return pullback(cotangent)
    grads = lax.map(one_section, (q_in, k_in, v_in, gate_in, incoming, conv_weight, bounds))
    return (jnp.roll(grads[0], -1, axis=0), jnp.roll(grads[1], -1, axis=0), jnp.roll(grads[2], -1, axis=0), jnp.roll(grads[3], -1, axis=0))
```

```python
import jax
import jax.numpy as jnp
from jax import lax
from jax.experimental import pallas as pl
from jax.experimental.pallas import tpu as pltpu
from jax.sharding import PartitionSpec as P

HEADS = 8
F = 16
DV = 128
T = 256
E = 160
N = 16
HALF = E // 2
WIDE = HEADS * DV
bf16 = jnp.bfloat16
f32 = jnp.float32
MESH = pl.DeviceIdType.MESH


def split(x):
    hi = x.astype(bf16)
    return hi, (x - hi.astype(f32)).astype(bf16)


def mm(a, b):
    return jnp.dot(a, b, preferred_element_type=f32)


def mm_nt(a, b):
    return lax.dot_general(a, b, (((1,), (1,)), ((), ())), preferred_element_type=f32)


def features(x, square):
    parts = [x, x * x * square]
    for r in range(1, 8):
        parts.append(x * pltpu.roll(x, r, axis=0))
    parts.append(x[:8] * x[8:])
    row = lax.broadcasted_iota(jnp.int32, (8, x.shape[1]), 0)
    parts.append(jnp.where(row == 0, 1.0, 0.0))
    return jnp.concatenate(parts, axis=0)


def features_back(g, x, square):
    out = g[:16] + g[16:32] * x * square
    for r in range(1, 8):
        gr = g[16 + 16 * r : 32 + 16 * r]
        out = out + gr * pltpu.roll(x, r, axis=0) + pltpu.roll(gr * x, 16 - r, axis=0)
    g8 = g[144:152]
    return out + jnp.concatenate([g8 * x[8:], g8 * x[:8]], axis=0)


def body(
    bounds, q_hbm, k_hbm, v_hbm, gate_hbm, og_hbm, w_hbm,
    dq_out, dk_out, dv_out, dgate_out,
    q_in, k_in, v_in, gate_in, w_in, cot, tail, head_next,
    q_t, k_t, phiq_hi, phiq_lo, phik_hi, phik_lo, qt_hi, qt_lo, kt_hi, kt_lo,
    mask, mask_t, u_all, numden, inv_all, ga_all, dsl, mixed_all,
    gn_hi, gn_lo, z_hi, z_lo, gmix, dv_acc, dq_t, dk_t,
    norm_own, norm_got, norm_in, norm_col, gd_rows, bnorm_own, bnorm_got, bnorm_col,
    s_own, s_got, pre_send, pre_got, b_own, b_got, suf_send, suf_got,
    dq_stage, dk_stage, dv_stage, dgate_stage,
    in_sem, cot_ss, cot_rs, halo_ss, halo_rs,
    n_ss, n_rs, bn_ss, bn_rs, p1_ss, p1_rs, p2_ss, p2_rs, p3_ss, p3_rs, p4_ss, p4_rs,
    out_ss, out_rs,
):
    me = lax.axis_index("ctx")
    pipe = lax.axis_index("pipe")
    pipes = lax.axis_size("pipe")
    before_pipe = {"pipe": lax.rem(pipe + pipes - 1, pipes)}
    after_pipe = {"pipe": lax.rem(pipe + 1, pipes)}

    barrier = pltpu.get_barrier_semaphore()
    for d in range(1, N):
        pl.semaphore_signal(barrier, inc=1, device_id={"ctx": lax.rem(me + d, N)}, device_id_type=MESH)
    pl.semaphore_signal(barrier, inc=1, device_id=before_pipe, device_id_type=MESH)
    pl.semaphore_signal(barrier, inc=1, device_id=after_pipe, device_id_type=MESH)

    loads = [
        pltpu.make_async_copy(src, dst, in_sem.at[i])
        for i, (src, dst) in enumerate(
            ((k_hbm, k_in), (q_hbm, q_in), (v_hbm, v_in), (gate_hbm, gate_in), (w_hbm, w_in))
        )
    ]
    for c in loads:
        c.start()

    def remote(src, dst, ss, rs, dev):
        return pltpu.make_async_remote_copy(
            src_ref=src, dst_ref=dst, send_sem=ss, recv_sem=rs, device_id=dev, device_id_type=MESH
        )

    def peer(d):
        return {"ctx": lax.rem(me + d, N)}

    b = bounds[0, me]
    opening = lax.rem(b, T)
    lane_t = lax.broadcasted_iota(jnp.int32, (1, T), 1)
    before_row = jnp.where(lane_t < b, 1.0, 0.0)
    after_row = jnp.where(lane_t >= opening, 1.0, 0.0)
    keep = [jnp.where(bounds[0, j] < T, 0.0, 1.0) for j in range(N)]
    head_lane = lax.shift_right_logical(lax.broadcasted_iota(jnp.int32, (1, 128), 1), 4)
    lane128 = lax.broadcasted_iota(jnp.int32, (1, 128), 1)
    row8 = lax.broadcasted_iota(jnp.int32, (8, 1), 0)

    def head16(h):
        return pl.ds(pl.multiple_of(h * 16, 16), 16)

    def head128(h):
        return pl.ds(pl.multiple_of(h * 128, 128), 128)

    loads[0].wait()
    k_t[...] = jnp.transpose(k_in[...].astype(f32)) * 0.5

    def key_features(h, norm):
        phi = features(k_t[head16(h), :], 1.0) * after_row
        hi, lo = split(phi)
        phik_hi[h] = hi
        phik_lo[h] = lo
        row = jnp.broadcast_to(jnp.where(row8 == h, 1.0, 0.0), (8, T)).astype(bf16)
        return norm + mm_nt(row, hi) + mm_nt(row, lo)

    norm = lax.fori_loop(0, HEADS, key_features, jnp.zeros((8, E), f32))
    norm_own[...] = jnp.concatenate([norm, jnp.zeros((8, T - E), f32)], axis=1)

    pl.semaphore_wait(barrier, N + 1)
    sends = []

    def start(c):
        c.start()
        sends.append(c)

    def gather_start(own, got, ss, rs):
        for d in range(1, N):
            start(remote(own, got.at[me], ss.at[d], rs.at[d], peer(d)))
        got[me] = own[...]

    def gather_wait(own, got, ss, rs):
        for d in range(1, N):
            remote(own, got.at[lax.rem(me + N - d, N)], ss.at[d], rs.at[d], peer(d)).wait_recv()

    gather_start(norm_own, norm_got, n_ss, n_rs)
    start(remote(gate_hbm.at[pl.ds(T - 16, 16)], tail, halo_ss.at[0], halo_rs.at[0], peer(1)))
    cots = []
    for i in range(4):
        cols = pl.ds(i * 256, 256)
        c = remote(og_hbm.at[:, cols], cot.at[:, cols], cot_ss.at[i], cot_rs.at[i], before_pipe)
        start(c)
        cots.append(c)

    loads[2].wait()

    def local_state(h, carry):
        v = v_in[:, head128(h)]
        s = mm(phik_hi[h], v) + mm(phik_lo[h], v)
        s_own[2 * h] = s[:HALF]
        s_own[2 * h + 1] = s[HALF:]
        return carry

    lax.fori_loop(0, HEADS, local_state, 0)

    def spread_start(own, got, ss, rs):
        for d in range(1, N):
            to = lax.rem(me + d, N)
            start(remote(own.at[to], got.at[me], ss.at[d], rs.at[d], {"ctx": to}))
        got[me] = own[me]

    def spread_wait(own, got, ss, rs):
        for d in range(1, N):
            src = lax.rem(me + N - d, N)
            remote(own.at[src], got.at[src], ss.at[d], rs.at[d], {"ctx": src}).wait_recv()

    spread_start(s_own, s_got, p1_ss, p1_rs)

    loads[1].wait()
    q_t[...] = jnp.transpose(q_in[...].astype(f32)) * 0.5
    ti = lax.broadcasted_iota(jnp.int32, (T, T), 0)
    si = lax.broadcasted_iota(jnp.int32, (T, T), 1)
    t_new = jnp.where(ti >= b, 1, 0)
    s_new = jnp.where(si >= b, 1, 0)
    mask[...] = jnp.where((ti >= si) & (t_new == s_new), 1.0, 0.0)
    mask_t[...] = jnp.where((si >= ti) & (t_new == s_new), 1.0, 0.0)

    def query_head(h):
        return (jnp.where(head_lane == h, q_in[...].astype(f32), 0.0) * 0.25).astype(bf16)

    def value_and_one(h):
        return jnp.concatenate([v_in[:, head128(h)], jnp.ones((T, 128), bf16)], axis=1)

    def inside(h, carry):
        phi = features(q_t[head16(h), :], 0.5) * before_row
        hi, lo = split(phi)
        phiq_hi[h] = hi
        phiq_lo[h] = lo
        hi, lo = split(jnp.transpose(phi))
        qt_hi[h] = hi
        qt_lo[h] = lo
        u = 1.0 + mm_nt(query_head(h), k_in[...])
        u_all[h] = u
        hi, lo = split(mask[...] * (0.5 * u * u + 0.5))
        va = value_and_one(h)
        numden[h] = mm(hi, va) + mm(lo, va)
        return carry

    lax.fori_loop(0, HEADS, inside, 0)

    loads[3].wait()
    loads[4].wait()
    remote(gate_hbm.at[pl.ds(T - 16, 16)], tail, halo_ss.at[0], halo_rs.at[0], peer(1)).wait_recv()
    pos = lax.broadcasted_iota(jnp.int32, (T, 1), 0)
    row_new = jnp.where(pos >= b, 1, 0)
    prev = lax.rem(me + N - 1, N)
    prev_open = lax.rem(bounds[0, prev], T)
    has_prev = jnp.where(me > 0, 1.0, 0.0)
    tail254 = jnp.where(prev_open <= T - 2, has_prev, 0.0)

    def usable(j):
        same = jnp.where(jnp.where(pos - j >= b, 1, 0) == row_new, 1.0, 0.0)
        return jnp.where(pos - j >= 0, same, jnp.where(pos < b, 1.0, 0.0))

    use1, use2 = usable(1), usable(2)

    def conv(h, carry):
        cols = head128(h)
        g = gate_in[:, cols].astype(f32)
        last = tail[:, cols].astype(f32)
        r254 = last[14:15] * tail254
        r255 = last[15:16] * has_prev
        g1 = jnp.where(pos == 0, r255, pltpu.roll(g, 1, axis=0))
        g2 = jnp.where(pos == 0, r254, jnp.where(pos == 1, r255, pltpu.roll(g, 2, axis=0)))
        w = w_in[:, cols].astype(f32)
        mixed_all[:, cols] = w[0:1] * g + w[1:2] * (g1 * use1) + w[2:3] * (g2 * use2)
        return carry

    lax.fori_loop(0, HEADS, conv, 0)

    gather_wait(norm_own, norm_got, n_ss, n_rs)
    acc = jnp.zeros((8, T), f32)
    for j in range(N):
        acc = jnp.where(j < me, norm_got[j] + keep[j] * acc, acc)
    norm_in[...] = acc
    norm_col[...] = jnp.transpose(jnp.concatenate([acc, jnp.zeros((120, T), f32)], axis=0))
    for c in cots:
        c.wait_recv()

    def numer_grad(h, carry):
        cols = head128(h)
        n_hi, n_lo = split(jnp.broadcast_to(norm_in[pl.ds(h, 1), :E], (128, E)))
        den = (
            numden[h, :, 128:]
            + mm_nt(qt_hi[h], n_hi) + mm_nt(qt_hi[h], n_lo) + mm_nt(qt_lo[h], n_hi)
        )
        inv = 1.0 / den
        inv_all[h] = inv
        mixed = mixed_all[:, cols]
        sig = 1.0 / (1.0 + jnp.exp(-mixed))
        cs = cot[:, cols].astype(f32) * sig
        ga = cs * mixed
        ga_all[:, cols] = ga
        dsl[:, cols] = cs * (1.0 + mixed * (1.0 - sig))
        hi, lo = split(ga * inv)
        gn_hi[h] = hi
        gn_lo[h] = lo
        s = mm(phiq_hi[h], hi) + mm(phiq_hi[h], lo) + mm(phiq_lo[h], hi)
        b_own[2 * h] = s[:HALF]
        b_own[2 * h + 1] = s[HALF:]
        return carry

    lax.fori_loop(0, HEADS, numer_grad, 0)
    spread_start(b_own, b_got, p3_ss, p3_rs)

    spread_wait(s_own, s_got, p1_ss, p1_rs)
    acc = jnp.zeros((HALF, 128), f32)
    for j in range(N):
        pre_send[j] = acc
        if j < N - 1:
            acc = s_got[j] + keep[j] * acc
    spread_start(pre_send, pre_got, p2_ss, p2_rs)

    def value_grad(h, carry):
        ut = 1.0 + mm_nt(k_in[...], query_head(h))
        hi, lo = split(mask_t[...] * (0.5 * ut * ut + 0.5))
        dv_acc[:, head128(h)] = mm(hi, gn_hi[h]) + mm(hi, gn_lo[h]) + mm(lo, gn_hi[h])
        hi, lo = split(jnp.transpose(phik_hi[h].astype(f32) + phik_lo[h].astype(f32)))
        kt_hi[h] = hi
        kt_lo[h] = lo
        return carry

    lax.fori_loop(0, HEADS, value_grad, 0)

    spread_wait(b_own, b_got, p3_ss, p3_rs)
    acc = jnp.zeros((HALF, 128), f32)
    for j in reversed(range(N)):
        suf_send[j] = acc
        if j > 0:
            acc = b_got[j] + keep[j] * acc
    spread_start(suf_send, suf_got, p4_ss, p4_rs)

    spread_wait(pre_send, pre_got, p2_ss, p2_rs)

    def attended(h, bnorm):
        cols = head128(h)
        p_hi, p_lo = split(jnp.concatenate([pre_got[2 * h], pre_got[2 * h + 1]], axis=0))
        num = (
            numden[h, :, :128]
            + mm(qt_hi[h], p_hi) + mm(qt_hi[h], p_lo) + mm(qt_lo[h], p_hi)
        )
        inv = inv_all[h]
        y = num * inv
        gmix[:, cols] = dsl[:, cols] * y
        hi, lo = split(-(ga_all[:, cols] * inv * y))
        z_hi[h] = hi
        z_lo[h] = lo
        row = jnp.broadcast_to(jnp.where(row8 == h, 1.0, 0.0), (8, 128)).astype(bf16)
        gd = mm_nt(row, hi) + mm_nt(row, lo)
        gd_rows[h] = jnp.broadcast_to(jnp.sum(gd, axis=0, keepdims=True), (8, T))
        hi, lo = split(gd)
        return bnorm + mm_nt(hi, phiq_hi[h]) + mm_nt(hi, phiq_lo[h]) + mm_nt(lo, phiq_hi[h])

    bnorm = lax.fori_loop(0, HEADS, attended, jnp.zeros((8, E), f32))
    bnorm_own[...] = jnp.concatenate([bnorm, jnp.zeros((8, T - E), f32)], axis=1)
    gather_start(bnorm_own, bnorm_got, bn_ss, bn_rs)
    start(remote(gmix.at[pl.ds(0, 8)], head_next, halo_ss.at[1], halo_rs.at[1], peer(N - 1)))

    def scores_grad(h, carry):
        va = value_and_one(h)
        g_hi = jnp.concatenate([gn_hi[h], z_hi[h]], axis=1)
        g_lo = jnp.concatenate([gn_lo[h], z_lo[h]], axis=1)
        hi, lo = split((mm_nt(g_hi, va) + mm_nt(g_lo, va)) * (u_all[h] * mask[...]))
        qh = q_t[head16(h), :]
        kh = k_t[head16(h), :].astype(bf16)
        dk_t[head16(h), :] = mm(qh.astype(bf16), hi) + mm(qh.astype(bf16), lo)
        p_hi, p_lo = split(jnp.concatenate([pre_got[2 * h], pre_got[2 * h + 1]], axis=0))
        col = jnp.sum(jnp.where(lane128 == h, norm_col[:E], 0.0), axis=1, keepdims=True)
        g = (
            mm_nt(p_hi, gn_hi[h]) + mm_nt(p_hi, gn_lo[h]) + mm_nt(p_lo, gn_hi[h])
            + col * gd_rows[h, 0:1]
        )
        dq_t[head16(h), :] = (
            mm_nt(kh, hi) + mm_nt(kh, lo) + before_row * features_back(g, qh, 1.0)
        )
        return carry

    lax.fori_loop(0, HEADS, scores_grad, 0)
    dq_stage[...] = (jnp.transpose(dq_t[...]) * 0.5).astype(bf16)
    outs = [remote(dq_stage, dq_out, out_ss.at[0], out_rs.at[0], before_pipe)]
    start(outs[0])

    remote(gmix.at[pl.ds(0, 8)], head_next, halo_ss.at[1], halo_rs.at[1], peer(N - 1)).wait_recv()
    nxt = lax.rem(me + 1, N)
    b_next = bounds[0, nxt]
    has_next = jnp.where(me < N - 1, 1.0, 0.0)
    next0 = jnp.where(b_next > 0, has_next, 0.0)
    next1 = jnp.where(b_next > 1, has_next, 0.0)

    def usable_back(j):
        same = jnp.where(jnp.where(pos + j >= b, 1, 0) == row_new, 1.0, 0.0)
        return jnp.where(pos + j < T, same, jnp.where(pos >= opening, 1.0, 0.0))

    back1, back2 = usable_back(1), usable_back(2)

    def conv_back(h, carry):
        cols = head128(h)
        g = gmix[:, cols]
        nr = head_next[:, cols]
        r0 = nr[0:1] * next0
        r1 = nr[1:2] * next1
        g1 = jnp.where(pos == T - 1, r0, pltpu.roll(g, T - 1, axis=0))
        g2 = jnp.where(pos == T - 1, r1, jnp.where(pos == T - 2, r0, pltpu.roll(g, T - 2, axis=0)))
        w = w_in[:, cols].astype(f32)
        out = w[0:1] * g + w[1:2] * (g1 * back1) + w[2:3] * (g2 * back2)
        dgate_stage[:, cols] = out.astype(bf16)
        return carry

    lax.fori_loop(0, HEADS, conv_back, 0)
    outs.append(remote(dgate_stage, dgate_out, out_ss.at[1], out_rs.at[1], before_pipe))
    start(outs[1])

    gather_wait(bnorm_own, bnorm_got, bn_ss, bn_rs)
    acc = jnp.zeros((8, T), f32)
    for j in reversed(range(N)):
        acc = jnp.where(j > me, bnorm_got[j] + keep[j] * acc, acc)
    bnorm_col[...] = jnp.transpose(jnp.concatenate([acc, jnp.zeros((120, T), f32)], axis=0))
    spread_wait(suf_send, suf_got, p4_ss, p4_rs)

    def key_value_grad(h, carry):
        cols = head128(h)
        s_hi, s_lo = split(jnp.concatenate([suf_got[2 * h], suf_got[2 * h + 1]], axis=0))
        dv = (
            dv_acc[:, cols]
            + mm(kt_hi[h], s_hi) + mm(kt_hi[h], s_lo) + mm(kt_lo[h], s_hi)
        )
        dv_stage[:, cols] = dv.astype(bf16)
        v = v_in[:, cols]
        col = jnp.sum(jnp.where(lane128 == h, bnorm_col[:E], 0.0), axis=1, keepdims=True)
        g = mm_nt(s_hi, v) + mm_nt(s_lo, v) + col
        dk_t[head16(h), :] += after_row * features_back(g, k_t[head16(h), :], 2.0)
        return carry

    for i in range(4):
        lax.fori_loop(2 * i, 2 * i + 2, key_value_grad, 0)
        cols = pl.ds(i * 256, 256)
        outs.append(remote(dv_stage.at[:, cols], dv_out.at[:, cols], out_ss.at[3 + i], out_rs.at[3 + i], before_pipe))
        start(outs[-1])
    dk_stage[...] = (jnp.transpose(dk_t[...]) * 0.5).astype(bf16)
    outs.append(remote(dk_stage, dk_out, out_ss.at[2], out_rs.at[2], before_pipe))
    start(outs[-1])

    for c in sends:
        c.wait_send()
    for c in outs:
        c.wait_recv()


def on_device(q_in, k_in, v_in, gate_in, out_grad, conv_weight, bounds):
    def vm(shape, dtype=f32):
        return pltpu.VMEM(shape, dtype)

    def sems(n):
        return pltpu.SemaphoreType.DMA((n,))

    any_spec = pl.BlockSpec(memory_space=pl.ANY)
    big = (N, HALF, 128)
    heads = (HEADS, T, 128)
    scratch = [
        vm((T, 128), bf16), vm((T, 128), bf16), vm((T, WIDE), bf16), vm((T, WIDE), bf16),
        vm((3, WIDE), bf16), vm((T, WIDE), bf16), vm((16, WIDE), bf16), vm((8, WIDE)),
        vm((128, T)), vm((128, T)),
        *[vm((HEADS, E, T), bf16)] * 4,
        *[vm((HEADS, T, E), bf16)] * 4,
        vm((T, T)), vm((T, T)), vm((HEADS, T, T)), vm((HEADS, T, 256)), vm(heads),
        vm((T, WIDE)), vm((T, WIDE)), vm((T, WIDE)),
        vm(heads, bf16), vm(heads, bf16), vm(heads, bf16), vm(heads, bf16),
        vm((T, WIDE)), vm((T, WIDE)), vm((128, T)), vm((128, T)),
        vm((8, T)), vm((N, 8, T)), vm((8, T)), vm((T, 128)), vm((HEADS, 8, T)),
        vm((8, T)), vm((N, 8, T)), vm((T, 128)),
        *[vm(big)] * 8,
        vm((T, 128), bf16), vm((T, 128), bf16), vm((T, WIDE), bf16), vm((T, WIDE), bf16),
        sems(5), sems(4), sems(4), sems(2), sems(2),
        *[sems(N)] * 12,
        sems(7), sems(7),
    ]
    narrow = jax.ShapeDtypeStruct((T, HEADS * F), bf16)
    wide = jax.ShapeDtypeStruct((T, WIDE), bf16)
    dq, dk, dv, dgate = pl.pallas_call(
        body,
        out_shape=(narrow, narrow, wide, wide),
        in_specs=[pl.BlockSpec(memory_space=pltpu.SMEM)] + [any_spec] * 6,
        out_specs=(any_spec,) * 4,
        scratch_shapes=scratch,
        compiler_params=pltpu.CompilerParams(
            collective_id=0, has_side_effects=True, vmem_limit_bytes=60 * 1024 * 1024
        ),
        name="section_backward",
    )(bounds, q_in[0], k_in[0], v_in[0], gate_in[0], out_grad[0], conv_weight[0])
    return dq[None], dk[None], dv[None], dgate[None]


def solution(mesh):
    tokens = P("pipe", "ctx", None)
    return jax.shard_map(
        on_device,
        mesh=mesh,
        in_specs=(tokens,) * 5 + (P("pipe", None, None), P("pipe", None)),
        out_specs=(tokens,) * 4,
        check_vma=False,
    )
```

```python
import jax
import jax.numpy as jnp
from jax import lax
from jax.experimental import pallas as pl
from jax.experimental.pallas import tpu as pltpu
from jax.sharding import PartitionSpec as P

HEADS = 8
F = 16
DV = 128
T = 256
E = 160
N = 16
HALF = E // 2
WIDE = HEADS * DV
bf16 = jnp.bfloat16
f32 = jnp.float32
MESH = pl.DeviceIdType.MESH


def split(x):
    hi = x.astype(bf16)
    return hi, (x - hi.astype(f32)).astype(bf16)


def mm(a, b):
    return jnp.dot(a, b, preferred_element_type=f32)


def mm_nt(a, b):
    return lax.dot_general(a, b, (((1,), (1,)), ((), ())), preferred_element_type=f32)


def features(x, square):
    parts = [x, x * x * square]
    for r in range(1, 8):
        parts.append(x * pltpu.roll(x, r, axis=0))
    parts.append(x[:8] * x[8:])
    row = lax.broadcasted_iota(jnp.int32, (8, x.shape[1]), 0)
    parts.append(jnp.where(row == 0, 1.0, 0.0))
    return jnp.concatenate(parts, axis=0)


def features_back(g, x, square):
    out = g[:16] + g[16:32] * x * square
    for r in range(1, 8):
        gr = g[16 + 16 * r : 32 + 16 * r]
        out = out + gr * pltpu.roll(x, r, axis=0) + pltpu.roll(gr * x, 16 - r, axis=0)
    g8 = g[144:152]
    return out + jnp.concatenate([g8 * x[8:], g8 * x[:8]], axis=0)


def body(
    bounds, q_hbm, k_hbm, v_hbm, gate_hbm, og_hbm, w_hbm,
    dq_out, dk_out, dv_out, dgate_out,
    q_in, k_in, v_in, gate_in, w_in, cot, tail, head_next,
    q_t, k_t, phiq_hi, phiq_lo, phik_hi, phik_lo, qt_hi, qt_lo, kt_hi, kt_lo,
    mask, mask_t, u_all, numden, inv_all, ga_all, dsl, silu,
    gn_hi, gn_lo, mu_hi, mu_lo, ku_t, gmix, dv_acc, dq_t, dk_t,
    norm_own, norm_got, norm_in, norm_col, gd_rows, bnorm_own, bnorm_got, bnorm_col,
    s_own, s_got, pre_send, pre_got, b_own, b_got, suf_send, suf_got,
    dq_stage, dk_stage, dv_stage, dgate_stage,
    in_sem, cot_ss, cot_rs, halo_ss, halo_rs,
    n_ss, n_rs, bn_ss, bn_rs, p1_ss, p1_rs, p2_ss, p2_rs, p3_ss, p3_rs, p4_ss, p4_rs,
    out_ss, out_rs,
):
    me = lax.axis_index("ctx")
    pipe = lax.axis_index("pipe")
    pipes = lax.axis_size("pipe")
    before_pipe = {"pipe": lax.rem(pipe + pipes - 1, pipes)}
    after_pipe = {"pipe": lax.rem(pipe + 1, pipes)}

    barrier = pltpu.get_barrier_semaphore()
    for d in range(1, N):
        pl.semaphore_signal(barrier, inc=1, device_id={"ctx": lax.rem(me + d, N)}, device_id_type=MESH)
    pl.semaphore_signal(barrier, inc=1, device_id=before_pipe, device_id_type=MESH)
    pl.semaphore_signal(barrier, inc=1, device_id=after_pipe, device_id_type=MESH)

    loads = [
        pltpu.make_async_copy(src, dst, in_sem.at[i])
        for i, (src, dst) in enumerate(
            ((k_hbm, k_in), (q_hbm, q_in), (v_hbm, v_in), (gate_hbm, gate_in), (w_hbm, w_in))
        )
    ]
    for c in loads:
        c.start()

    def remote(src, dst, ss, rs, dev):
        return pltpu.make_async_remote_copy(
            src_ref=src, dst_ref=dst, send_sem=ss, recv_sem=rs, device_id=dev, device_id_type=MESH
        )

    def peer(d):
        return {"ctx": lax.rem(me + d, N)}

    b = bounds[0, me]
    opening = lax.rem(b, T)
    lane_t = lax.broadcasted_iota(jnp.int32, (1, T), 1)
    before_row = jnp.where(lane_t < b, 1.0, 0.0)
    after_row = jnp.where(lane_t >= opening, 1.0, 0.0)
    keep = [jnp.where(bounds[0, j] < T, 0.0, 1.0) for j in range(N)]
    head_lane = lax.shift_right_logical(lax.broadcasted_iota(jnp.int32, (1, 128), 1), 4)
    lane128 = lax.broadcasted_iota(jnp.int32, (1, 128), 1)
    row8 = lax.broadcasted_iota(jnp.int32, (8, 1), 0)

    def by_groups(fn, carry, before=None, after=None, size=4):
        def group(g, carry):
            index = [g * size + r for r in range(size)]
            for i in index if before else ():
                before(i)
            for i in index:
                carry = fn(i, carry)
            for i in index if after else ():
                after(i)
            return carry

        return lax.fori_loop(0, HEADS // size, group, carry)

    def head16(h):
        return pl.ds(pl.multiple_of(h * 16, 16), 16)

    def head128(h):
        return pl.ds(pl.multiple_of(h * 128, 128), 128)

    loads[0].wait()
    k_t[...] = jnp.transpose(k_in[...].astype(f32)) * 0.5

    def key_features(h, norm):
        phi = features(k_t[head16(h), :], 1.0) * after_row
        hi, lo = split(phi)
        phik_hi[h] = hi
        phik_lo[h] = lo
        row = jnp.broadcast_to(jnp.where(row8 == h, 1.0, 0.0), (8, T)).astype(bf16)
        return norm + mm_nt(row, hi) + mm_nt(row, lo)

    norm = by_groups(key_features, jnp.zeros((8, E), f32))
    norm_own[...] = jnp.concatenate([norm, jnp.zeros((8, T - E), f32)], axis=1)

    pl.semaphore_wait(barrier, N + 1)
    sends = []

    def start(c):
        c.start()
        sends.append(c)

    def gather_start(own, got, ss, rs):
        for d in range(1, N):
            start(remote(own, got.at[me], ss.at[d], rs.at[d], peer(d)))
        got[me] = own[...]

    def gather_wait(own, got, ss, rs):
        for d in range(1, N):
            remote(own, got.at[lax.rem(me + N - d, N)], ss.at[d], rs.at[d], peer(d)).wait_recv()

    gather_start(norm_own, norm_got, n_ss, n_rs)
    start(remote(gate_hbm.at[pl.ds(T - 16, 16)], tail, halo_ss.at[0], halo_rs.at[0], peer(1)))

    def cot_piece(i):
        cols = head128(lax.rem(i + lax.shift_right_logical(me, 1), HEADS))
        return remote(og_hbm.at[:, cols], cot.at[:, cols], cot_ss.at[i], cot_rs.at[i], before_pipe)

    for i in range(HEADS):
        start(cot_piece(i))

    loads[2].wait()

    def chunk_start(own, got, ss, rs, j):
        @pl.when(j != me)
        def _():
            remote(own.at[j], got.at[me], ss.at[j], rs.at[me], {"ctx": j}).start()

        @pl.when(j == me)
        def _():
            got[me] = own[me]

    def spread_start(own, got, ss, rs):
        for d in range(1, N):
            to = lax.rem(me + d, N)
            remote(own.at[to], got.at[me], ss.at[to], rs.at[me], {"ctx": to}).start()
        got[me] = own[me]

    def spread_wait(own, got, ss, rs):
        for d in range(1, N):
            src = lax.rem(me + N - d, N)
            remote(own.at[src], got.at[src], ss.at[src], rs.at[src], {"ctx": src}).wait_recv()

    def spread_sent(own, got, ss, rs):
        for d in range(1, N):
            to = lax.rem(me + d, N)
            remote(own.at[to], got.at[me], ss.at[to], rs.at[me], {"ctx": to}).wait_send()

    def turn(i):
        return lax.rem(i + lax.shift_right_logical(me, 1), HEADS)

    def local_state(i, carry):
        h = turn(i)
        v = v_in[:, head128(h)]
        s = mm(phik_hi[h], v) + mm(phik_lo[h], v)
        s_own[2 * h] = s[:HALF]
        s_own[2 * h + 1] = s[HALF:]
        return carry

    def state_sends(i):
        chunk_start(s_own, s_got, p1_ss, p1_rs, 2 * turn(i))
        chunk_start(s_own, s_got, p1_ss, p1_rs, 2 * turn(i) + 1)

    by_groups(local_state, 0, after=state_sends)

    loads[1].wait()
    q_t[...] = jnp.transpose(q_in[...].astype(f32)) * 0.5
    ti = lax.broadcasted_iota(jnp.int32, (T, T), 0)
    si = lax.broadcasted_iota(jnp.int32, (T, T), 1)
    t_new = jnp.where(ti >= b, 1, 0)
    s_new = jnp.where(si >= b, 1, 0)
    mask[...] = jnp.where((ti >= si) & (t_new == s_new), 1.0, 0.0)
    mask_t[...] = jnp.where((si >= ti) & (t_new == s_new), 1.0, 0.0)

    def query_head(h):
        return (jnp.where(head_lane == h, q_in[...].astype(f32), 0.0) * 0.25).astype(bf16)

    def value_and_one(h):
        return jnp.concatenate([v_in[:, head128(h)], jnp.ones((T, 128), bf16)], axis=1)

    def inside(h, carry):
        phi = features(q_t[head16(h), :], 0.5) * before_row
        hi, lo = split(phi)
        phiq_hi[h] = hi
        phiq_lo[h] = lo
        hi, lo = split(jnp.transpose(phi))
        qt_hi[h] = hi
        qt_lo[h] = lo
        u = 1.0 + mm_nt(query_head(h), k_in[...])
        u_all[h] = u
        hi, lo = split(mask[...] * (0.5 * u * u + 0.5))
        va = value_and_one(h)
        numden[h] = mm(hi, va) + mm(lo, va)
        return carry

    by_groups(inside, 0)

    loads[3].wait()
    loads[4].wait()
    remote(gate_hbm.at[pl.ds(T - 16, 16)], tail, halo_ss.at[0], halo_rs.at[0], peer(1)).wait_recv()
    pos = lax.broadcasted_iota(jnp.int32, (T, 1), 0)
    row_new = jnp.where(pos >= b, 1, 0)
    prev = lax.rem(me + N - 1, N)
    prev_open = lax.rem(bounds[0, prev], T)
    has_prev = jnp.where(me > 0, 1.0, 0.0)
    tail254 = jnp.where(prev_open <= T - 2, has_prev, 0.0)

    def usable(j):
        same = jnp.where(jnp.where(pos - j >= b, 1, 0) == row_new, 1.0, 0.0)
        return jnp.where(pos - j >= 0, same, jnp.where(pos < b, 1.0, 0.0))

    use1, use2 = usable(1), usable(2)

    def conv(h, carry):
        cols = head128(h)
        g = gate_in[:, cols].astype(f32)
        last = tail[:, cols].astype(f32)
        r254 = last[14:15] * tail254
        r255 = last[15:16] * has_prev
        g1 = jnp.where(pos == 0, r255, pltpu.roll(g, 1, axis=0))
        g2 = jnp.where(pos == 0, r254, jnp.where(pos == 1, r255, pltpu.roll(g, 2, axis=0)))
        w = w_in[:, cols].astype(f32)
        mixed = w[0:1] * g + w[1:2] * (g1 * use1) + w[2:3] * (g2 * use2)
        sig = 1.0 / (1.0 + jnp.exp(-mixed))
        silu[:, cols] = mixed * sig
        dsl[:, cols] = sig * (1.0 + mixed * (1.0 - sig))
        return carry

    by_groups(conv, 0)

    gather_wait(norm_own, norm_got, n_ss, n_rs)
    acc = jnp.zeros((8, T), f32)
    for j in range(N):
        acc = jnp.where(j < me, norm_got[j] + keep[j] * acc, acc)
    norm_in[...] = acc
    norm_col[...] = jnp.transpose(jnp.concatenate([acc, jnp.zeros((120, T), f32)], axis=0))

    def numer_grad(i, carry):
        h = turn(i)
        cols = head128(h)
        n_hi, n_lo = split(jnp.broadcast_to(norm_in[pl.ds(h, 1), :E], (128, E)))
        den = (
            numden[h, :, 128:]
            + mm_nt(qt_hi[h], n_hi) + mm_nt(qt_hi[h], n_lo) + mm_nt(qt_lo[h], n_hi)
        )
        inv = 1.0 / den
        inv_all[h] = inv
        ga = cot[:, cols].astype(f32) * silu[:, cols]
        ga_all[:, cols] = ga
        hi, lo = split(ga * inv)
        gn_hi[h] = hi
        gn_lo[h] = lo
        s = mm(phiq_hi[h], hi) + mm(phiq_hi[h], lo) + mm(phiq_lo[h], hi)
        b_own[2 * h] = s[:HALF]
        b_own[2 * h + 1] = s[HALF:]
        return carry

    def grad_sends(i):
        chunk_start(b_own, b_got, p3_ss, p3_rs, 2 * turn(i))
        chunk_start(b_own, b_got, p3_ss, p3_rs, 2 * turn(i) + 1)

    by_groups(numer_grad, 0, before=lambda i: cot_piece(i).wait_recv(), after=grad_sends)

    spread_wait(s_own, s_got, p1_ss, p1_rs)
    acc = jnp.zeros((HALF, 128), f32)
    for j in range(N):
        pre_send[j] = acc
        if j < N - 1:
            acc = s_got[j] + keep[j] * acc
    spread_start(pre_send, pre_got, p2_ss, p2_rs)

    def value_grad(h, carry):
        ut = 1.0 + mm_nt(k_in[...], query_head(h))
        hi, lo = split(mask_t[...] * (0.5 * ut * ut + 0.5))
        dv_acc[:, head128(h)] = mm(hi, gn_hi[h]) + mm(hi, gn_lo[h]) + mm(lo, gn_hi[h])
        hi, lo = split(jnp.transpose(phik_hi[h].astype(f32) + phik_lo[h].astype(f32)))
        kt_hi[h] = hi
        kt_lo[h] = lo
        v = v_in[:, head128(h)]
        mu = u_all[h] * mask[...]
        hi, lo = split((mm_nt(gn_hi[h], v) + mm_nt(gn_lo[h], v)) * mu)
        qh = q_t[head16(h), :].astype(bf16)
        kh = k_t[head16(h), :].astype(bf16)
        dk_t[head16(h), :] = mm(qh, hi) + mm(qh, lo)
        dq_t[head16(h), :] = mm_nt(kh, hi) + mm_nt(kh, lo)
        hi, lo = split(mu)
        mu_hi[h] = hi
        mu_lo[h] = lo
        ku_t[head16(h), :] = mm_nt(kh, hi) + mm_nt(kh, lo)
        return carry

    by_groups(value_grad, 0)

    spread_wait(b_own, b_got, p3_ss, p3_rs)
    acc = jnp.zeros((HALF, 128), f32)
    for j in reversed(range(N)):
        suf_send[j] = acc
        if j > 0:
            acc = b_got[j] + keep[j] * acc
    spread_start(suf_send, suf_got, p4_ss, p4_rs)

    spread_wait(pre_send, pre_got, p2_ss, p2_rs)

    def attended(h, bnorm):
        cols = head128(h)
        p_hi, p_lo = split(jnp.concatenate([pre_got[2 * h], pre_got[2 * h + 1]], axis=0))
        num = (
            numden[h, :, :128]
            + mm(qt_hi[h], p_hi) + mm(qt_hi[h], p_lo) + mm(qt_lo[h], p_hi)
        )
        inv = inv_all[h]
        y = num * inv
        gmix[:, cols] = cot[:, cols].astype(f32) * dsl[:, cols] * y
        hi, lo = split(-(ga_all[:, cols] * inv * y))
        row = jnp.broadcast_to(jnp.where(row8 == h, 1.0, 0.0), (8, 128)).astype(bf16)
        gd = mm_nt(row, hi) + mm_nt(row, lo)
        gd_rows[h] = jnp.broadcast_to(jnp.sum(gd, axis=0, keepdims=True), (8, T))
        hi, lo = split(gd)
        return bnorm + mm_nt(hi, phiq_hi[h]) + mm_nt(hi, phiq_lo[h]) + mm_nt(lo, phiq_hi[h])

    bnorm = by_groups(attended, jnp.zeros((8, E), f32))
    bnorm_own[...] = jnp.concatenate([bnorm, jnp.zeros((8, T - E), f32)], axis=1)
    gather_start(bnorm_own, bnorm_got, bn_ss, bn_rs)
    start(remote(gmix.at[pl.ds(0, 8)], head_next, halo_ss.at[1], halo_rs.at[1], peer(N - 1)))

    remote(gmix.at[pl.ds(0, 8)], head_next, halo_ss.at[1], halo_rs.at[1], peer(N - 1)).wait_recv()
    nxt = lax.rem(me + 1, N)
    b_next = bounds[0, nxt]
    has_next = jnp.where(me < N - 1, 1.0, 0.0)
    next0 = jnp.where(b_next > 0, has_next, 0.0)
    next1 = jnp.where(b_next > 1, has_next, 0.0)

    def usable_back(j):
        same = jnp.where(jnp.where(pos + j >= b, 1, 0) == row_new, 1.0, 0.0)
        return jnp.where(pos + j < T, same, jnp.where(pos >= opening, 1.0, 0.0))

    back1, back2 = usable_back(1), usable_back(2)

    def conv_back(h, carry):
        cols = head128(h)
        g = gmix[:, cols]
        nr = head_next[:, cols]
        r0 = nr[0:1] * next0
        r1 = nr[1:2] * next1
        g1 = jnp.where(pos == T - 1, r0, pltpu.roll(g, T - 1, axis=0))
        g2 = jnp.where(pos == T - 1, r1, jnp.where(pos == T - 2, r0, pltpu.roll(g, T - 2, axis=0)))
        w = w_in[:, cols].astype(f32)
        out = w[0:1] * g + w[1:2] * (g1 * back1) + w[2:3] * (g2 * back2)
        dgate_stage[:, cols] = out.astype(bf16)
        return carry

    by_groups(conv_back, 0)
    dgate_copy = remote(dgate_stage, dgate_out, out_ss.at[9], out_rs.at[9], before_pipe)
    start(dgate_copy)

    def scores_grad(h, carry):
        qh = q_t[head16(h), :]
        gd = gd_rows[h, 0:1]
        hi, lo = split(qh * gd)
        dk_t[head16(h), :] += mm(hi, mu_hi[h]) + mm(hi, mu_lo[h]) + mm(lo, mu_hi[h])
        p_hi, p_lo = split(jnp.concatenate([pre_got[2 * h], pre_got[2 * h + 1]], axis=0))
        col = jnp.sum(jnp.where(lane128 == h, norm_col[:E], 0.0), axis=1, keepdims=True)
        g = mm_nt(p_hi, gn_hi[h]) + mm_nt(p_hi, gn_lo[h]) + mm_nt(p_lo, gn_hi[h]) + col * gd
        dq_t[head16(h), :] += ku_t[head16(h), :] * gd + before_row * features_back(g, qh, 1.0)
        return carry

    by_groups(scores_grad, 0)
    dq_stage[...] = (jnp.transpose(dq_t[...]) * 0.5).astype(bf16)
    dq_copy = remote(dq_stage, dq_out, out_ss.at[8], out_rs.at[8], before_pipe)
    start(dq_copy)

    gather_wait(bnorm_own, bnorm_got, bn_ss, bn_rs)
    acc = jnp.zeros((8, T), f32)
    for j in reversed(range(N)):
        acc = jnp.where(j > me, bnorm_got[j] + keep[j] * acc, acc)
    bnorm_col[...] = jnp.transpose(jnp.concatenate([acc, jnp.zeros((120, T), f32)], axis=0))
    spread_wait(suf_send, suf_got, p4_ss, p4_rs)

    def dv_copy(h):
        cols = head128(h)
        return remote(dv_stage.at[:, cols], dv_out.at[:, cols], out_ss.at[h], out_rs.at[h], before_pipe)

    def key_value_grad(h, carry):
        cols = head128(h)
        s_hi, s_lo = split(jnp.concatenate([suf_got[2 * h], suf_got[2 * h + 1]], axis=0))
        dv = (
            dv_acc[:, cols]
            + mm(kt_hi[h], s_hi) + mm(kt_hi[h], s_lo) + mm(kt_lo[h], s_hi)
        )
        dv_stage[:, cols] = dv.astype(bf16)
        v = v_in[:, cols]
        col = jnp.sum(jnp.where(lane128 == h, bnorm_col[:E], 0.0), axis=1, keepdims=True)
        g = mm_nt(s_hi, v) + mm_nt(s_lo, v) + col
        dk_t[head16(h), :] += after_row * features_back(g, k_t[head16(h), :], 2.0)
        return carry

    by_groups(key_value_grad, 0, after=lambda i: dv_copy(i).start())
    dk_stage[...] = (jnp.transpose(dk_t[...]) * 0.5).astype(bf16)
    dk_copy = remote(dk_stage, dk_out, out_ss.at[10], out_rs.at[10], before_pipe)
    start(dk_copy)

    for c in sends:
        c.wait_send()
    spread_sent(s_own, s_got, p1_ss, p1_rs)
    spread_sent(pre_send, pre_got, p2_ss, p2_rs)
    spread_sent(b_own, b_got, p3_ss, p3_rs)
    spread_sent(suf_send, suf_got, p4_ss, p4_rs)
    for h in range(HEADS):
        dv_copy(h).wait_send()
    for c in [dq_copy, dgate_copy, dk_copy] + [dv_copy(h) for h in range(HEADS)]:
        c.wait_recv()


def on_device(q_in, k_in, v_in, gate_in, out_grad, conv_weight, bounds):
    def vm(shape, dtype=f32):
        return pltpu.VMEM(shape, dtype)

    def sems(n):
        return pltpu.SemaphoreType.DMA((n,))

    any_spec = pl.BlockSpec(memory_space=pl.ANY)
    big = (N, HALF, 128)
    heads = (HEADS, T, 128)
    scratch = [
        vm((T, 128), bf16), vm((T, 128), bf16), vm((T, WIDE), bf16), vm((T, WIDE), bf16),
        vm((3, WIDE), bf16), vm((T, WIDE), bf16), vm((16, WIDE), bf16), vm((8, WIDE)),
        vm((128, T)), vm((128, T)),
        *[vm((HEADS, E, T), bf16)] * 4,
        *[vm((HEADS, T, E), bf16)] * 4,
        vm((T, T)), vm((T, T)), vm((HEADS, T, T)), vm((HEADS, T, 256)), vm(heads),
        vm((T, WIDE)), vm((T, WIDE)), vm((T, WIDE)),
        vm(heads, bf16), vm(heads, bf16), vm((HEADS, T, T), bf16), vm((HEADS, T, T), bf16), vm((128, T)),
        vm((T, WIDE)), vm((T, WIDE)), vm((128, T)), vm((128, T)),
        vm((8, T)), vm((N, 8, T)), vm((8, T)), vm((T, 128)), vm((HEADS, 8, T)),
        vm((8, T)), vm((N, 8, T)), vm((T, 128)),
        *[vm(big)] * 8,
        vm((T, 128), bf16), vm((T, 128), bf16), vm((T, WIDE), bf16), vm((T, WIDE), bf16),
        sems(5), sems(HEADS), sems(HEADS), sems(2), sems(2),
        *[sems(N)] * 12,
        sems(11), sems(11),
    ]
    narrow = (T, HEADS * F)
    wide = (T, WIDE)
    shapes = (narrow, narrow, wide, wide)
    results = pl.pallas_call(
        body,
        out_shape=tuple(pltpu.VMEM(x, bf16) for x in shapes),
        in_specs=[pl.BlockSpec(memory_space=pltpu.SMEM)] + [any_spec] * 6,
        out_specs=(pl.BlockSpec(memory_space=pltpu.VMEM),) * 4,
        scratch_shapes=scratch,
        compiler_params=pltpu.CompilerParams(
            collective_id=0, has_side_effects=True, vmem_limit_bytes=56 * 1024 * 1024
        ),
        name="section_backward",
    )(bounds, q_in[0], k_in[0], v_in[0], gate_in[0], out_grad[0], conv_weight[0])
    return tuple(x[None] for x in results)


def solution(mesh):
    tokens = P("pipe", "ctx", None)
    return jax.shard_map(
        on_device,
        mesh=mesh,
        in_specs=(tokens,) * 5 + (P("pipe", None, None), P("pipe", None)),
        out_specs=(tokens,) * 4,
        check_vma=False,
    )
```

```python
import jax
import jax.numpy as jnp
from jax import lax
from jax.experimental import pallas as pl
from jax.experimental.pallas import tpu as pltpu
from jax.sharding import PartitionSpec as P

HEADS = 8
F = 16
DV = 128
T = 256
E = 160
N = 16
HALF = E // 2
WIDE = HEADS * DV
bf16 = jnp.bfloat16
f32 = jnp.float32
MESH = pl.DeviceIdType.MESH


def split(x):
    hi = x.astype(bf16)
    return hi, (x - hi.astype(f32)).astype(bf16)


def mm(a, b):
    return jnp.dot(a, b, preferred_element_type=f32)


def mm_nt(a, b):
    return lax.dot_general(a, b, (((1,), (1,)), ((), ())), preferred_element_type=f32)


def features(x, square):
    parts = [x, x * x * square]
    for r in range(1, 8):
        parts.append(x * pltpu.roll(x, r, axis=0))
    parts.append(x[:8] * x[8:])
    row = lax.broadcasted_iota(jnp.int32, (8, x.shape[1]), 0)
    parts.append(jnp.where(row == 0, 1.0, 0.0))
    return jnp.concatenate(parts, axis=0)


def features_back(g, x, square):
    out = g[:16] + g[16:32] * x * square
    for r in range(1, 8):
        gr = g[16 + 16 * r : 32 + 16 * r]
        out = out + gr * pltpu.roll(x, r, axis=0) + pltpu.roll(gr * x, 16 - r, axis=0)
    g8 = g[144:152]
    return out + jnp.concatenate([g8 * x[8:], g8 * x[:8]], axis=0)


def body(
    bounds, q_hbm, k_hbm, v_hbm, gate_hbm, og_hbm, w_hbm,
    dq_out, dk_out, dv_out, dgate_out,
    q_in, k_in, v_in, gate_in, w_in, cot, tail, head_next,
    q_t, k_t, phiq_hi, phiq_lo, phik_hi, phik_lo, qt_hi, qt_lo, kt_hi, kt_lo,
    mask, mask_t, u_all, numden, inv_all, ga_all, dsl, silu,
    gn_hi, gn_lo, mu_hi, mu_lo, ku_t, gmix, dv_acc, dq_t, dk_t,
    norm_own, norm_got, norm_in, norm_col, gd_rows, bnorm_own, bnorm_got, bnorm_col,
    s_own, s_got, pre_send, pre_got, b_own, b_got, suf_send, suf_got,
    dq_stage, dk_stage, dv_stage, dgate_stage,
    in_sem, cot_ss, cot_rs, halo_ss, halo_rs,
    n_ss, n_rs, bn_ss, bn_rs, p1_ss, p1_rs, p2_ss, p2_rs, p3_ss, p3_rs, p4_ss, p4_rs,
    out_ss, out_rs,
):
    me = lax.axis_index("ctx")
    pipe = lax.axis_index("pipe")
    pipes = lax.axis_size("pipe")
    before_pipe = {"pipe": lax.rem(pipe + pipes - 1, pipes)}
    after_pipe = {"pipe": lax.rem(pipe + 1, pipes)}

    barrier = pltpu.get_barrier_semaphore()
    for d in range(1, N):
        pl.semaphore_signal(barrier, inc=1, device_id={"ctx": lax.rem(me + d, N)}, device_id_type=MESH)
    pl.semaphore_signal(barrier, inc=1, device_id=before_pipe, device_id_type=MESH)
    pl.semaphore_signal(barrier, inc=1, device_id=after_pipe, device_id_type=MESH)

    loads = [
        pltpu.make_async_copy(src, dst, in_sem.at[i])
        for i, (src, dst) in enumerate(
            ((k_hbm, k_in), (q_hbm, q_in), (v_hbm, v_in), (gate_hbm, gate_in), (w_hbm, w_in))
        )
    ]
    for c in loads:
        c.start()

    def remote(src, dst, ss, rs, dev):
        return pltpu.make_async_remote_copy(
            src_ref=src, dst_ref=dst, send_sem=ss, recv_sem=rs, device_id=dev, device_id_type=MESH
        )

    def peer(d):
        return {"ctx": lax.rem(me + d, N)}

    b = bounds[0, me]
    opening = lax.rem(b, T)
    lane_t = lax.broadcasted_iota(jnp.int32, (1, T), 1)
    before_row = jnp.where(lane_t < b, 1.0, 0.0)
    after_row = jnp.where(lane_t >= opening, 1.0, 0.0)
    keep = [jnp.where(bounds[0, j] < T, 0.0, 1.0) for j in range(N)]
    head_lane = lax.shift_right_logical(lax.broadcasted_iota(jnp.int32, (1, 128), 1), 4)
    lane128 = lax.broadcasted_iota(jnp.int32, (1, 128), 1)
    row8 = lax.broadcasted_iota(jnp.int32, (8, 1), 0)

    def by_groups(fn, carry, before=None, after=None, size=4):
        def group(g, carry):
            index = [g * size + r for r in range(size)]
            for i in index if before else ():
                before(i)
            for i in index:
                carry = fn(i, carry)
            for i in index if after else ():
                after(i)
            return carry

        return lax.fori_loop(0, HEADS // size, group, carry)

    def head16(h):
        return pl.ds(pl.multiple_of(h * 16, 16), 16)

    def head128(h):
        return pl.ds(pl.multiple_of(h * 128, 128), 128)

    loads[0].wait()
    k_t[...] = jnp.transpose(k_in[...].astype(f32)) * 0.5

    def key_features(h, norm):
        phi = features(k_t[head16(h), :], 1.0) * after_row
        hi, lo = split(phi)
        phik_hi[h] = hi
        phik_lo[h] = lo
        row = jnp.broadcast_to(jnp.where(row8 == h, 1.0, 0.0), (8, T)).astype(bf16)
        return norm + mm_nt(row, hi) + mm_nt(row, lo)

    norm = by_groups(key_features, jnp.zeros((8, E), f32))
    norm_own[...] = jnp.concatenate([norm, jnp.zeros((8, T - E), f32)], axis=1)

    pl.semaphore_wait(barrier, N + 1)
    sends = []

    def start(c):
        c.start()
        sends.append(c)

    def gather_start(own, got, ss, rs):
        for d in range(1, N):
            start(remote(own, got.at[me], ss.at[d], rs.at[d], peer(d)))
        got[me] = own[...]

    def gather_wait(own, got, ss, rs):
        for d in range(1, N):
            remote(own, got.at[lax.rem(me + N - d, N)], ss.at[d], rs.at[d], peer(d)).wait_recv()

    gather_start(norm_own, norm_got, n_ss, n_rs)
    start(remote(gate_hbm.at[pl.ds(T - 16, 16)], tail, halo_ss.at[0], halo_rs.at[0], peer(1)))

    def cot_piece(i):
        cols = head128(lax.rem(i + lax.shift_right_logical(me, 1), HEADS))
        return remote(og_hbm.at[:, cols], cot.at[:, cols], cot_ss.at[i], cot_rs.at[i], before_pipe)

    for i in range(HEADS):
        start(cot_piece(i))

    loads[2].wait()

    def chunk_start(own, got, ss, rs, j):
        @pl.when(j != me)
        def _():
            remote(own.at[j], got.at[me], ss.at[j], rs.at[me], {"ctx": j}).start()

        @pl.when(j == me)
        def _():
            got[me] = own[me]

    def spread_start(own, got, ss, rs):
        for d in range(1, N):
            to = lax.rem(me + d, N)
            remote(own.at[to], got.at[me], ss.at[to], rs.at[me], {"ctx": to}).start()
        got[me] = own[me]

    def spread_wait(own, got, ss, rs):
        for d in range(1, N):
            src = lax.rem(me + N - d, N)
            remote(own.at[src], got.at[src], ss.at[src], rs.at[src], {"ctx": src}).wait_recv()

    def spread_sent(own, got, ss, rs):
        for d in range(1, N):
            to = lax.rem(me + d, N)
            remote(own.at[to], got.at[me], ss.at[to], rs.at[me], {"ctx": to}).wait_send()

    def turn(i):
        return lax.rem(i + lax.shift_right_logical(me, 1), HEADS)

    def local_state(i, carry):
        h = turn(i)
        v = v_in[:, head128(h)]
        s = mm(phik_hi[h], v) + mm(phik_lo[h], v)
        s_own[2 * h] = s[:HALF]
        s_own[2 * h + 1] = s[HALF:]
        return carry

    def state_sends(i):
        chunk_start(s_own, s_got, p1_ss, p1_rs, 2 * turn(i))
        chunk_start(s_own, s_got, p1_ss, p1_rs, 2 * turn(i) + 1)

    by_groups(local_state, 0, after=state_sends)

    loads[1].wait()
    q_t[...] = jnp.transpose(q_in[...].astype(f32)) * 0.5
    ti = lax.broadcasted_iota(jnp.int32, (T, T), 0)
    si = lax.broadcasted_iota(jnp.int32, (T, T), 1)
    t_new = jnp.where(ti >= b, 1, 0)
    s_new = jnp.where(si >= b, 1, 0)
    mask[...] = jnp.where((ti >= si) & (t_new == s_new), 1.0, 0.0)
    mask_t[...] = jnp.where((si >= ti) & (t_new == s_new), 1.0, 0.0)

    def query_head(h):
        return (jnp.where(head_lane == h, q_in[...].astype(f32), 0.0) * 0.25).astype(bf16)

    def value_and_one(h):
        return jnp.concatenate([v_in[:, head128(h)], jnp.ones((T, 128), bf16)], axis=1)

    def inside(h, carry):
        phi = features(q_t[head16(h), :], 0.5) * before_row
        hi, lo = split(phi)
        phiq_hi[h] = hi
        phiq_lo[h] = lo
        hi, lo = split(jnp.transpose(phi))
        qt_hi[h] = hi
        qt_lo[h] = lo
        u = 1.0 + mm_nt(query_head(h), k_in[...])
        u_all[h] = u
        hi, lo = split(mask[...] * (0.5 * u * u + 0.5))
        va = value_and_one(h)
        numden[h] = mm(hi, va) + mm(lo, va)
        return carry

    by_groups(inside, 0)

    loads[3].wait()
    loads[4].wait()
    remote(gate_hbm.at[pl.ds(T - 16, 16)], tail, halo_ss.at[0], halo_rs.at[0], peer(1)).wait_recv()
    pos = lax.broadcasted_iota(jnp.int32, (T, 1), 0)
    row_new = jnp.where(pos >= b, 1, 0)
    prev = lax.rem(me + N - 1, N)
    prev_open = lax.rem(bounds[0, prev], T)
    has_prev = jnp.where(me > 0, 1.0, 0.0)
    tail254 = jnp.where(prev_open <= T - 2, has_prev, 0.0)

    def usable(j):
        same = jnp.where(jnp.where(pos - j >= b, 1, 0) == row_new, 1.0, 0.0)
        return jnp.where(pos - j >= 0, same, jnp.where(pos < b, 1.0, 0.0))

    use1, use2 = usable(1), usable(2)

    def conv(h, carry):
        cols = head128(h)
        g = gate_in[:, cols].astype(f32)
        last = tail[:, cols].astype(f32)
        r254 = last[14:15] * tail254
        r255 = last[15:16] * has_prev
        g1 = jnp.where(pos == 0, r255, pltpu.roll(g, 1, axis=0))
        g2 = jnp.where(pos == 0, r254, jnp.where(pos == 1, r255, pltpu.roll(g, 2, axis=0)))
        w = w_in[:, cols].astype(f32)
        mixed = w[0:1] * g + w[1:2] * (g1 * use1) + w[2:3] * (g2 * use2)
        sig = 1.0 / (1.0 + jnp.exp(-mixed))
        silu[:, cols] = mixed * sig
        dsl[:, cols] = sig * (1.0 + mixed * (1.0 - sig))
        return carry

    by_groups(conv, 0)

    gather_wait(norm_own, norm_got, n_ss, n_rs)
    acc = jnp.zeros((8, T), f32)
    for j in range(N):
        acc = jnp.where(j < me, norm_got[j] + keep[j] * acc, acc)
    norm_in[...] = acc
    norm_col[...] = jnp.transpose(jnp.concatenate([acc, jnp.zeros((120, T), f32)], axis=0))

    def numer_grad(i, carry):
        h = turn(i)
        cols = head128(h)
        n_hi, n_lo = split(jnp.broadcast_to(norm_in[pl.ds(h, 1), :E], (128, E)))
        den = (
            numden[h, :, 128:]
            + mm_nt(qt_hi[h], n_hi) + mm_nt(qt_hi[h], n_lo) + mm_nt(qt_lo[h], n_hi)
        )
        inv = 1.0 / den
        inv_all[h] = inv
        ga = cot[:, cols].astype(f32) * silu[:, cols]
        ga_all[:, cols] = ga
        hi, lo = split(ga * inv)
        gn_hi[h] = hi
        gn_lo[h] = lo
        s = mm(phiq_hi[h], hi) + mm(phiq_hi[h], lo) + mm(phiq_lo[h], hi)
        b_own[2 * h] = s[:HALF]
        b_own[2 * h + 1] = s[HALF:]
        return carry

    def grad_sends(i):
        chunk_start(b_own, b_got, p3_ss, p3_rs, 2 * turn(i))
        chunk_start(b_own, b_got, p3_ss, p3_rs, 2 * turn(i) + 1)

    by_groups(numer_grad, 0, before=lambda i: cot_piece(i).wait_recv(), after=grad_sends)

    spread_wait(s_own, s_got, p1_ss, p1_rs)
    acc = jnp.zeros((HALF, 128), f32)
    for j in range(N):
        pre_send[j] = acc
        if j < N - 1:
            acc = s_got[j] + keep[j] * acc
    spread_start(pre_send, pre_got, p2_ss, p2_rs)

    def value_grad(h, carry):
        ut = 1.0 + mm_nt(k_in[...], query_head(h))
        hi, lo = split(mask_t[...] * (0.5 * ut * ut + 0.5))
        dv_acc[:, head128(h)] = mm(hi, gn_hi[h]) + mm(hi, gn_lo[h]) + mm(lo, gn_hi[h])
        hi, lo = split(jnp.transpose(phik_hi[h].astype(f32) + phik_lo[h].astype(f32)))
        kt_hi[h] = hi
        kt_lo[h] = lo
        v = v_in[:, head128(h)]
        mu = u_all[h] * mask[...]
        hi, lo = split((mm_nt(gn_hi[h], v) + mm_nt(gn_lo[h], v)) * mu)
        qh = q_t[head16(h), :].astype(bf16)
        kh = k_t[head16(h), :].astype(bf16)
        dk_t[head16(h), :] = mm(qh, hi) + mm(qh, lo)
        dq_t[head16(h), :] = mm_nt(kh, hi) + mm_nt(kh, lo)
        hi, lo = split(mu)
        mu_hi[h] = hi
        mu_lo[h] = lo
        ku_t[head16(h), :] = mm_nt(kh, hi) + mm_nt(kh, lo)
        return carry

    by_groups(value_grad, 0)

    spread_wait(b_own, b_got, p3_ss, p3_rs)
    acc = jnp.zeros((HALF, 128), f32)
    for j in reversed(range(N)):
        suf_send[j] = acc
        if j > 0:
            acc = b_got[j] + keep[j] * acc
    spread_start(suf_send, suf_got, p4_ss, p4_rs)

    spread_wait(pre_send, pre_got, p2_ss, p2_rs)

    def attended(h, bnorm):
        cols = head128(h)
        p_hi, p_lo = split(jnp.concatenate([pre_got[2 * h], pre_got[2 * h + 1]], axis=0))
        num = (
            numden[h, :, :128]
            + mm(qt_hi[h], p_hi) + mm(qt_hi[h], p_lo) + mm(qt_lo[h], p_hi)
        )
        inv = inv_all[h]
        y = num * inv
        gmix[:, cols] = cot[:, cols].astype(f32) * dsl[:, cols] * y
        hi, lo = split(-(ga_all[:, cols] * inv * y))
        row = jnp.broadcast_to(jnp.where(row8 == h, 1.0, 0.0), (8, 128)).astype(bf16)
        gd = mm_nt(row, hi) + mm_nt(row, lo)
        gd_rows[h] = jnp.broadcast_to(jnp.sum(gd, axis=0, keepdims=True), (8, T))
        hi, lo = split(gd)
        return bnorm + mm_nt(hi, phiq_hi[h]) + mm_nt(hi, phiq_lo[h]) + mm_nt(lo, phiq_hi[h])

    bnorm = by_groups(attended, jnp.zeros((8, E), f32))
    bnorm_own[...] = jnp.concatenate([bnorm, jnp.zeros((8, T - E), f32)], axis=1)
    gather_start(bnorm_own, bnorm_got, bn_ss, bn_rs)
    start(remote(gmix.at[pl.ds(0, 8)], head_next, halo_ss.at[1], halo_rs.at[1], peer(N - 1)))

    remote(gmix.at[pl.ds(0, 8)], head_next, halo_ss.at[1], halo_rs.at[1], peer(N - 1)).wait_recv()
    nxt = lax.rem(me + 1, N)
    b_next = bounds[0, nxt]
    has_next = jnp.where(me < N - 1, 1.0, 0.0)
    next0 = jnp.where(b_next > 0, has_next, 0.0)
    next1 = jnp.where(b_next > 1, has_next, 0.0)

    def usable_back(j):
        same = jnp.where(jnp.where(pos + j >= b, 1, 0) == row_new, 1.0, 0.0)
        return jnp.where(pos + j < T, same, jnp.where(pos >= opening, 1.0, 0.0))

    back1, back2 = usable_back(1), usable_back(2)

    def conv_back(h, carry):
        cols = head128(h)
        g = gmix[:, cols]
        nr = head_next[:, cols]
        r0 = nr[0:1] * next0
        r1 = nr[1:2] * next1
        g1 = jnp.where(pos == T - 1, r0, pltpu.roll(g, T - 1, axis=0))
        g2 = jnp.where(pos == T - 1, r1, jnp.where(pos == T - 2, r0, pltpu.roll(g, T - 2, axis=0)))
        w = w_in[:, cols].astype(f32)
        out = w[0:1] * g + w[1:2] * (g1 * back1) + w[2:3] * (g2 * back2)
        dgate_stage[:, cols] = out.astype(bf16)
        return carry

    by_groups(conv_back, 0)
    dgate_copy = remote(dgate_stage, dgate_out, out_ss.at[9], out_rs.at[9], before_pipe)
    start(dgate_copy)

    def scores_grad(h, carry):
        qh = q_t[head16(h), :]
        gd = gd_rows[h, 0:1]
        hi, lo = split(qh * gd)
        dk_t[head16(h), :] += mm(hi, mu_hi[h]) + mm(hi, mu_lo[h]) + mm(lo, mu_hi[h])
        p_hi, p_lo = split(jnp.concatenate([pre_got[2 * h], pre_got[2 * h + 1]], axis=0))
        col = jnp.sum(jnp.where(lane128 == h, norm_col[:E], 0.0), axis=1, keepdims=True)
        g = mm_nt(p_hi, gn_hi[h]) + mm_nt(p_hi, gn_lo[h]) + mm_nt(p_lo, gn_hi[h]) + col * gd
        dq_t[head16(h), :] += ku_t[head16(h), :] * gd + before_row * features_back(g, qh, 1.0)
        return carry

    by_groups(scores_grad, 0)
    dq_stage[...] = (jnp.transpose(dq_t[...]) * 0.5).astype(bf16)
    dq_copy = remote(dq_stage, dq_out, out_ss.at[8], out_rs.at[8], before_pipe)
    start(dq_copy)

    spread_wait(suf_send, suf_got, p4_ss, p4_rs)

    def dv_copy(h):
        cols = head128(h)
        return remote(dv_stage.at[:, cols], dv_out.at[:, cols], out_ss.at[h], out_rs.at[h], before_pipe)

    def suffix(h):
        return split(jnp.concatenate([suf_got[2 * h], suf_got[2 * h + 1]], axis=0))

    def value_out(h, carry):
        cols = head128(h)
        s_hi, s_lo = suffix(h)
        dv = (
            dv_acc[:, cols]
            + mm(kt_hi[h], s_hi) + mm(kt_hi[h], s_lo) + mm(kt_lo[h], s_hi)
        )
        dv_stage[:, cols] = dv.astype(bf16)
        return carry

    by_groups(value_out, 0, after=lambda i: dv_copy(i).start())

    gather_wait(bnorm_own, bnorm_got, bn_ss, bn_rs)
    acc = jnp.zeros((8, T), f32)
    for j in reversed(range(N)):
        acc = jnp.where(j > me, bnorm_got[j] + keep[j] * acc, acc)
    bnorm_col[...] = jnp.transpose(jnp.concatenate([acc, jnp.zeros((120, T), f32)], axis=0))

    def key_out(h, carry):
        s_hi, s_lo = suffix(h)
        v = v_in[:, head128(h)]
        col = jnp.sum(jnp.where(lane128 == h, bnorm_col[:E], 0.0), axis=1, keepdims=True)
        g = mm_nt(s_hi, v) + mm_nt(s_lo, v) + col
        dk_t[head16(h), :] += after_row * features_back(g, k_t[head16(h), :], 2.0)
        return carry

    by_groups(key_out, 0)
    dk_stage[...] = (jnp.transpose(dk_t[...]) * 0.5).astype(bf16)
    dk_copy = remote(dk_stage, dk_out, out_ss.at[10], out_rs.at[10], before_pipe)
    start(dk_copy)

    for c in sends:
        c.wait_send()
    spread_sent(s_own, s_got, p1_ss, p1_rs)
    spread_sent(pre_send, pre_got, p2_ss, p2_rs)
    spread_sent(b_own, b_got, p3_ss, p3_rs)
    spread_sent(suf_send, suf_got, p4_ss, p4_rs)
    for h in range(HEADS):
        dv_copy(h).wait_send()
    for c in [dq_copy, dgate_copy, dk_copy] + [dv_copy(h) for h in range(HEADS)]:
        c.wait_recv()


def on_device(q_in, k_in, v_in, gate_in, out_grad, conv_weight, bounds):
    def vm(shape, dtype=f32):
        return pltpu.VMEM(shape, dtype)

    def sems(n):
        return pltpu.SemaphoreType.DMA((n,))

    any_spec = pl.BlockSpec(memory_space=pl.ANY)
    big = (N, HALF, 128)
    heads = (HEADS, T, 128)
    scratch = [
        vm((T, 128), bf16), vm((T, 128), bf16), vm((T, WIDE), bf16), vm((T, WIDE), bf16),
        vm((3, WIDE), bf16), vm((T, WIDE), bf16), vm((16, WIDE), bf16), vm((8, WIDE)),
        vm((128, T)), vm((128, T)),
        *[vm((HEADS, E, T), bf16)] * 4,
        *[vm((HEADS, T, E), bf16)] * 4,
        vm((T, T)), vm((T, T)), vm((HEADS, T, T)), vm((HEADS, T, 256)), vm(heads),
        vm((T, WIDE)), vm((T, WIDE)), vm((T, WIDE)),
        vm(heads, bf16), vm(heads, bf16), vm((HEADS, T, T), bf16), vm((HEADS, T, T), bf16), vm((128, T)),
        vm((T, WIDE)), vm((T, WIDE)), vm((128, T)), vm((128, T)),
        vm((8, T)), vm((N, 8, T)), vm((8, T)), vm((T, 128)), vm((HEADS, 8, T)),
        vm((8, T)), vm((N, 8, T)), vm((T, 128)),
        *[vm(big)] * 8,
        vm((T, 128), bf16), vm((T, 128), bf16), vm((T, WIDE), bf16), vm((T, WIDE), bf16),
        sems(5), sems(HEADS), sems(HEADS), sems(2), sems(2),
        *[sems(N)] * 12,
        sems(11), sems(11),
    ]
    narrow = (T, HEADS * F)
    wide = (T, WIDE)
    shapes = (narrow, narrow, wide, wide)
    results = pl.pallas_call(
        body,
        out_shape=tuple(pltpu.VMEM(x, bf16) for x in shapes),
        in_specs=[pl.BlockSpec(memory_space=pltpu.SMEM)] + [any_spec] * 6,
        out_specs=(pl.BlockSpec(memory_space=pltpu.VMEM),) * 4,
        scratch_shapes=scratch,
        compiler_params=pltpu.CompilerParams(
            collective_id=0, has_side_effects=True, vmem_limit_bytes=56 * 1024 * 1024
        ),
        name="section_backward",
    )(bounds, q_in[0], k_in[0], v_in[0], gate_in[0], out_grad[0], conv_weight[0])
    return tuple(x[None] for x in results)


def solution(mesh):
    tokens = P("pipe", "ctx", None)
    return jax.shard_map(
        on_device,
        mesh=mesh,
        in_specs=(tokens,) * 5 + (P("pipe", None, None), P("pipe", None)),
        out_specs=(tokens,) * 4,
        check_vma=False,
    )
```
